32 devices in a mesh: seq: 8 (over y, x, core), ffn: 4 (over z).
Axes of the slice: x: 2, y: 2, z: 4, core: 2. Of those that a mesh axis runs over, the one named last changes fastest.
Arguments:
- attn_in: float32 [1024, 2, 1024], P('seq', None, 'ffn'), may hold values from -0.25 to 0.25
- attn_out: float32 [1024, 1024], P('ffn', 'seq'), may hold values from -0.5 to 0.5
- ffn_in: float32 [1024, 4096], P('seq', 'ffn'), may hold values from -0.1875 to 0.1875
- ffn_out: float32 [4096, 1024], P('ffn', 'seq'), may hold values from -0.09375 to 0.09375
- tables: float32 [672, 1024], P(None, ('seq', 'ffn'))
- norm_params: float32 [6, 1024], P(None, ('seq', 'ffn'))
- m_attn_in: float32 [1024, 2, 1024], P('seq', None, 'ffn'), may hold values from -2.2888184e-05 to 2.2888184e-05
- m_attn_out: float32 [1024, 1024], P('ffn', 'seq'), may hold values from -2.2888184e-05 to 2.2888184e-05
- m_ffn_in: float32 [1024, 4096], P('seq', 'ffn'), may hold values from -2.2888184e-05 to 2.2888184e-05
- m_ffn_out: float32 [4096, 1024], P('ffn', 'seq'), may hold values from -2.2888184e-05 to 2.2888184e-05
- m_tables: float32 [672, 1024], P(None, ('seq', 'ffn')), may hold values from -2.2888184e-05 to 2.2888184e-05
- m_norm_params: float32 [6, 1024], P(None, ('seq', 'ffn')), may hold values from -2.2888184e-05 to 2.2888184e-05
- v_attn_in: float32 [1024, 2, 1024], P('seq', None, 'ffn'), may hold values from 2.1674416e-13 to 8.6697663e-13
- v_attn_out: float32 [1024, 1024], P('ffn', 'seq'), may hold values from 2.1674416e-13 to 8.6697663e-13
- v_ffn_in: float32 [1024, 4096], P('seq', 'ffn'), may hold values from 2.1674416e-13 to 8.6697663e-13
- v_ffn_out: float32 [4096, 1024], P('ffn', 'seq'), may hold values from 2.1674416e-13 to 8.6697663e-13
- v_tables: float32 [672, 1024], P(None, ('seq', 'ffn')), may hold values from 2.1674416e-13 to 8.6697663e-13
- v_norm_params: float32 [6, 1024], P(None, ('seq', 'ffn')), may hold values from 2.1674416e-13 to 8.6697663e-13
- tokens: int32 [2, 4096], P(None, 'seq'), may hold values from 0 to 255
- targets: int32 [2, 4096], P(None, ('seq', 'ffn')), may hold values from 0 to 255
- loss_mask: int32 [2, 4096], replicated, may hold values from 0 to 1, as said below
- lengths: int32 [2], replicated, may hold values from 1024 to 4096, as said below
- buckets: int32 [2, 2, 4096, 1], replicated, may hold values from 0 to 255; in each aligned block of 512 rows (0 to 511, 512 to 1023, ..., all dimensions but the last counted through in order) at most 4 rows name the same one
Outputs:
- new_attn_in: float32 [1024, 2, 1024], P('seq', None, 'ffn')
- new_attn_out: float32 [1024, 1024], P('ffn', 'seq')
- new_ffn_in: float32 [1024, 4096], P('seq', 'ffn')
- new_ffn_out: float32 [4096, 1024], P('ffn', 'seq')
- new_tables: float32 [672, 1024], P(None, ('seq', 'ffn'))
- new_norm_params: float32 [6, 1024], P(None, ('seq', 'ffn'))
- new_m_attn_in: float32 [1024, 2, 1024], P('seq', None, 'ffn')
- new_m_attn_out: float32 [1024, 1024], P('ffn', 'seq')
- new_m_ffn_in: float32 [1024, 4096], P('seq', 'ffn')
- new_m_ffn_out: float32 [4096, 1024], P('ffn', 'seq')
- new_m_tables: float32 [672, 1024], P(None, ('seq', 'ffn'))
- new_m_norm_params: float32 [6, 1024], P(None, ('seq', 'ffn'))
- new_v_attn_in: float32 [1024, 2, 1024], P('seq', None, 'ffn')
- new_v_attn_out: float32 [1024, 1024], P('ffn', 'seq')
- new_v_ffn_in: float32 [1024, 4096], P('seq', 'ffn')
- new_v_ffn_out: float32 [4096, 1024], P('ffn', 'seq')
- new_v_tables: float32 [672, 1024], P(None, ('seq', 'ffn'))
- new_v_norm_params: float32 [6, 1024], P(None, ('seq', 'ffn'))
- grad_norm: float32 [], replicated
- loss_total: float32 [], replicated
The draws below stay inside these ranges and needn't reach their ends.
Inputs may be any that keep to these rules, and one draw needn't show every extreme that they name: `buckets`: in each aligned block of 512 positions of one sequence and one round, no bucket is named more than 4 times, a bound that some block reaches. `lengths`: one sequence of every draw has the full length 4096. `loss_mask`: position 0 of every sequence counts.
All inputs are finite; a program needn't handle non-finite values.
Results may differ from the reference program's by a relative error of at most 0.017.
Values may be sent and summed in bfloat16 or wider, within the bound.
No kernel may reach another device: no remote copies, remote signals or barrier semaphores. Data moves between devices by JAX's collectives and lax.ppermute only.
A program may use at most 192 MiB of HBM per device.

```python
import math
import jax
import jax.numpy as jnp
import numpy as np
from jax import lax

D = 1024
HEADS = 8
HEAD = 128
FF = 4096
VOCAB = 256
BUCKETS = 256
CAP = 4
ROUNDS = 2
POS_LO = 128
STEP = 10
SEQS = 2
SEG = 512
LENGTH = 4096
TROWS = 672
N_SEQ = 8


def draw_tables(key, part):
    noise_base = jax.random.normal(key, (TROWS, D), jnp.float32)
    row_index = jnp.arange(TROWS)[:, None]
    factor = jnp.where(row_index < VOCAB, 0.5, jnp.where(row_index < 2 * VOCAB, 2.0 / math.sqrt(D), 0.3))
    return noise_base * factor


def draw_norm_params(key, part):
    gain_rows = jax.random.uniform(jax.random.fold_in(key, 1), (6, D), jnp.float32, 0.5, 1.5)
    shifts = 0.2 * jax.random.normal(jax.random.fold_in(key, 2), (6, D), jnp.float32)
    row_index = jnp.arange(6)[:, None]
    return jnp.where(row_index % 2 == 0, gain_rows, shifts)


def draw_lengths(key, part):
    drawn_len = jax.random.randint(jax.random.fold_in(key, 1), (SEQS,), LENGTH // 4, LENGTH + 1)
    full_index = jax.random.randint(jax.random.fold_in(key, 2), (), 0, SEQS)
    return jnp.where(jnp.arange(SEQS) == full_index, LENGTH, drawn_len).astype(jnp.int32)


def draw_loss_mask(key, part):
    levels = jax.random.randint(key, (SEQS, LENGTH), 0, 8)
    leading = jnp.arange(LENGTH)[None, :] == 0
    return jnp.where(leading | (levels > 0), 1, 0).astype(jnp.int32)


def place_ends(values, rng, smallest, top_value):
    longest = values.shape.index(max(values.shape))
    spots = []
    for shift in (0, 1):
        where = [jax.random.randint(jax.random.fold_in(rng, axis), (), 0, length) for axis, length in enumerate(values.shape)]
        where[longest] = (where[longest] + shift) % values.shape[longest]
        spots.append(tuple(where))
    return values.at[spots[0]].set(smallest).at[spots[1]].set(top_value)


def shard_levels(rng, dims, cuts, least, high):
    def one(dim, blocks):
        draws = jax.random.uniform(jax.random.fold_in(jax.random.fold_in(rng, 6), dim), (blocks,), jnp.float32, least / len(cuts), high / len(cuts))
        return jnp.repeat(jnp.exp(draws), dims[dim] // blocks).reshape((-1,) + (1,) * (len(dims) - dim - 1))

    level = one(*cuts[0])
    for cut in cuts[1:]:
        level = level * one(*cut)
    return level


def rank_table(number_of, slope):
    portions = [(1 << 20) // math.isqrt(standing ** slope) + 1 for standing in range(1, number_of + 1)]
    width = 1 + sum(portions) // (1 << 30)
    return np.cumsum(np.array([max(1, weight // width) for weight in portions]))


def skewed_ids(own_key, extent, number_of, skew):
    table = rank_table(number_of, skew)
    pick = jax.random.randint(jax.random.fold_in(own_key, 1), extent, 0, int(table[number_of - 1]))
    grade = jnp.searchsorted(jnp.asarray(table, jnp.int32), pick, side="right")
    return jax.random.permutation(jax.random.fold_in(own_key, 2), number_of)[grade].astype(jnp.int32)


def shared_out(own_key, own, number, rows, count, top, reach, lean):
    order = jax.random.permutation(own_key, count)
    crowded, usual = shares(count, rows * top, reach, lean, True), shares(count, rows * top, reach, lean, False)
    places = jnp.arange(count)

    def named(tallies, rotation):
        used = int((tallies > 0).sum())
        fixed = max(1, used // 4)
        passed = fixed + (places - fixed + rotation * (used - fixed)) % max(1, count - fixed)
        return jnp.zeros((count,), jnp.int32).at[order[jnp.where(places < fixed, places, passed)]].set(jnp.asarray(tallies, jnp.int32))

    tallies = jnp.where(number % 4 == 0, named(crowded, number // 4), named(usual, number - number // 4 - 1))
    mixed = jax.random.permutation(jax.random.fold_in(own, 3), count)
    source_of, taker = mixed[0:count // 2 * 2:2], mixed[1:count // 2 * 2:2]
    room = jnp.minimum(tallies[source_of] - 1, reach - tallies[taker]) // 2
    room = jnp.where((source_of == order[0]) | (taker == order[0]) | (tallies[taker] == 0), 0, jnp.maximum(room, 0))
    passed = jax.random.randint(jax.random.fold_in(own, 4), (count // 2,), 0, 1 << 20) % (room + 1)
    tallies = tallies.at[source_of].add(-passed).at[taker].add(passed)
    items = jnp.searchsorted(jnp.cumsum(tallies), jnp.arange(rows * top), side="right").astype(jnp.int32)
    grid = items.reshape(top, rows).T
    grid = grid[jax.random.permutation(jax.random.fold_in(own, 1), rows)]
    rotation = jax.random.randint(jax.random.fold_in(own, 2), (rows, 1), 0, top)
    return jnp.take_along_axis(grid, (jnp.arange(top)[None, :] + rotation) % top, axis=1)


def shares(number_of, total, most, slope, full):
    loads = [(1 << 20) // math.isqrt(grade ** slope) + 1 for grade in range(1, number_of + 1)]
    largest = most if full else min(most, max(-(-total // number_of), total * loads[0] // sum(loads)))
    least = 1 if total - largest >= number_of - 1 else 0
    given, surplus = [largest] + [least] * (number_of - 1), total - largest - least * (number_of - 1)
    while surplus > 0:
        free = [i for i in range(1, number_of) if given[i] < largest] or [i for i in range(1, number_of) if given[i] < most]
        mass, remaining = sum([loads[i] for i in free]), surplus
        for i in free:
            extra = min(most - given[i], max(1, remaining * loads[i] // mass), surplus)
            given[i] = given[i] + extra
            surplus = surplus - extra
    return np.array(given)


def noise(key, shape, width, bound, shards=(), held_as=jnp.bfloat16):
    values = width * jax.random.normal(key, shape, jnp.float32)
    if shards:
        values = values * shard_levels(key, shape, shards, -0.22, 0.18)
    return jnp.clip(values, -bound, bound).astype(held_as)


def setup_inputs(seed: int = 0) -> dict:
    key_of = jax.random.split(jax.random.key(seed), 24)
    attn_in = noise(key_of[0], (D, 2, HEADS * HEAD), (D // 2) ** -0.5, 0.25, ((0, 8), (2, 4)), jnp.float32)
    attn_out = noise(key_of[1], (HEADS * HEAD, D), (HEADS * HEAD // 8) ** -0.5, 0.5, ((0, 4), (1, 8)), jnp.float32)
    ffn_in = noise(key_of[2], (D, FF), D ** -0.5, 0.1875, ((0, 8), (1, 4)), jnp.float32)
    ffn_out = noise(key_of[3], (FF, D), FF ** -0.5, 0.09375, ((0, 4), (1, 8)), jnp.float32)
    tables = draw_tables(jax.random.fold_in(key_of[23], 71), 0)
    norm_params = draw_norm_params(jax.random.fold_in(key_of[23], 71), 0)
    m_attn_in = noise(key_of[6], (D, 2, HEADS * HEAD), (0.0055 * (D * (3 * D + 2 * FF)) ** -0.5), 2.288818359375e-05, ((0, 8), (2, 4)), jnp.float32)
    m_attn_out = noise(key_of[7], (HEADS * HEAD, D), (0.0055 * (D * (3 * D + 2 * FF)) ** -0.5), 2.288818359375e-05, ((0, 4), (1, 8)), jnp.float32)
    m_ffn_in = noise(key_of[8], (D, FF), (0.0055 * (D * (3 * D + 2 * FF)) ** -0.5), 2.288818359375e-05, ((0, 8), (1, 4)), jnp.float32)
    m_ffn_out = noise(key_of[9], (FF, D), (0.0055 * (D * (3 * D + 2 * FF)) ** -0.5), 2.288818359375e-05, ((0, 4), (1, 8)), jnp.float32)
    m_tables = noise(key_of[10], (TROWS, D), (0.0055 * (D * (3 * D + 2 * FF)) ** -0.5), 2.288818359375e-05, ((1, 32),), jnp.float32)
    m_norm_params = noise(key_of[11], (6, D), (0.0055 * (D * (3 * D + 2 * FF)) ** -0.5), 2.288818359375e-05, ((1, 32),), jnp.float32)
    v_attn_in = jnp.clip(jnp.exp(math.log(8.669766293767367e-13) - 1.3862944 * jax.random.uniform(key_of[12], (D, 2, HEADS * HEAD), jnp.float32) ** shard_levels(key_of[12], (D, 2, HEADS * HEAD), ((0, 8), (2, 4)), -0.2, 0.2)), 2.1674415734418417e-13, 8.669766293767367e-13)
    v_attn_out = jnp.clip(jnp.exp(math.log(8.669766293767367e-13) - 1.3862944 * jax.random.uniform(key_of[13], (HEADS * HEAD, D), jnp.float32) ** shard_levels(key_of[13], (HEADS * HEAD, D), ((0, 4), (1, 8)), -0.2, 0.2)), 2.1674415734418417e-13, 8.669766293767367e-13)
    v_ffn_in = jnp.clip(jnp.exp(math.log(8.669766293767367e-13) - 1.3862944 * jax.random.uniform(key_of[14], (D, FF), jnp.float32) ** shard_levels(key_of[14], (D, FF), ((0, 8), (1, 4)), -0.2, 0.2)), 2.1674415734418417e-13, 8.669766293767367e-13)
    v_ffn_out = jnp.clip(jnp.exp(math.log(8.669766293767367e-13) - 1.3862944 * jax.random.uniform(key_of[15], (FF, D), jnp.float32) ** shard_levels(key_of[15], (FF, D), ((0, 4), (1, 8)), -0.2, 0.2)), 2.1674415734418417e-13, 8.669766293767367e-13)
    v_tables = jnp.clip(jnp.exp(math.log(8.669766293767367e-13) - 1.3862944 * jax.random.uniform(key_of[16], (TROWS, D), jnp.float32) ** shard_levels(key_of[16], (TROWS, D), ((1, 32),), -0.2, 0.2)), 2.1674415734418417e-13, 8.669766293767367e-13)
    v_norm_params = jnp.clip(jnp.exp(math.log(8.669766293767367e-13) - 1.3862944 * jax.random.uniform(key_of[17], (6, D), jnp.float32) ** shard_levels(key_of[17], (6, D), ((1, 32),), -0.2, 0.2)), 2.1674415734418417e-13, 8.669766293767367e-13)
    tokens = place_ends(skewed_ids(key_of[18], (SEQS, LENGTH), VOCAB, 2), jax.random.fold_in(key_of[18], 3), 0, VOCAB - 1).astype(jnp.int32)
    targets = place_ends(skewed_ids(key_of[19], (SEQS, LENGTH), VOCAB, 2), jax.random.fold_in(key_of[19], 3), 0, VOCAB - 1).astype(jnp.int32)
    loss_mask = draw_loss_mask(jax.random.fold_in(key_of[23], 71), 0)
    lengths = draw_lengths(jax.random.fold_in(key_of[23], 71), 0)
    buckets_keys = jax.random.split(jax.random.fold_in(key_of[22], 1), SEQS * ROUNDS * LENGTH // SEG)
    buckets_turns = jax.random.permutation(jax.random.fold_in(key_of[22], 3), SEQS * ROUNDS * LENGTH // SEG)
    buckets = jax.vmap(lambda own, number: shared_out(jax.random.fold_in(key_of[22], 2), own, number, SEG, BUCKETS, 1, CAP, 1))(buckets_keys, buckets_turns).reshape((SEQS, ROUNDS, LENGTH, 1))
    return {"attn_in": attn_in, "attn_out": attn_out, "ffn_in": ffn_in, "ffn_out": ffn_out, "tables": tables, "norm_params": norm_params, "m_attn_in": m_attn_in, "m_attn_out": m_attn_out, "m_ffn_in": m_ffn_in, "m_ffn_out": m_ffn_out, "m_tables": m_tables, "m_norm_params": m_norm_params, "v_attn_in": v_attn_in, "v_attn_out": v_attn_out, "v_ffn_in": v_ffn_in, "v_ffn_out": v_ffn_out, "v_tables": v_tables, "v_norm_params": v_norm_params, "tokens": tokens, "targets": targets, "loss_mask": loss_mask, "lengths": lengths, "buckets": buckets}


PRECISE = lax.Precision.HIGHEST
PENALTY = 10000.0
MASKED = -1000000000.0
LN_EPS = 1e-05
KEY_EPS = 1e-06
CLIP_NORM = 0.05
BETA_ONE = 0.9
BETA_TWO = 0.999
ADAM_EPS = 1e-08
WEIGHT_DECAY = 0.01
STEP_RATES = (0.1, 0.2, 0.1, 0.05, 0.5, 0.5)
LOG_TWO = 0.6931471805599453

@jax.custom_vjp
def low(v):
    return lax.optimization_barrier(v.astype(jnp.bfloat16)).astype(jnp.float32)

@jax.custom_vjp
def low_back(v):
    return v

def low_keep(v):
    return (low(v), None)

def low_pass(kept, grad):
    return (grad,)

def back_keep(v):
    return (v, None)

def back_low(kept, grad):
    return (low(grad),)
low.defvjp(low_keep, low_pass)
low_back.defvjp(back_keep, back_low)

def layer_norm(values, scale_row, shift_row):
    average = lax.optimization_barrier(jnp.mean(values, axis=-1, keepdims=True))
    centred = values - average
    inv_std = lax.rsqrt(lax.optimization_barrier(jnp.mean(centred * centred, axis=-1, keepdims=True)) + LN_EPS)
    return centred * inv_std * scale_row + shift_row

def matmul(left, right):
    return jnp.dot(left, right, precision=PRECISE, preferred_element_type=jnp.float32)

def bucket_slots(bucket_ids):
    position = jnp.arange(LENGTH, dtype=jnp.int32)
    sorted_order = jnp.argsort(bucket_ids * LENGTH + position).astype(jnp.int32)
    matches = bucket_ids[:, None] == jnp.arange(BUCKETS, dtype=jnp.int32)[None, :]
    counts = lax.optimization_barrier(jnp.sum(matches.astype(jnp.int32), axis=0)).astype(jnp.int32)
    starts = (jnp.cumsum(counts) - counts).astype(jnp.int32)
    column = jnp.arange(N_SEQ * CAP, dtype=jnp.int32)
    slot_rows = (starts[:, None] + column[None, :]).astype(jnp.int32)
    member = sorted_order[jnp.minimum(slot_rows, LENGTH - 1)]
    slot_pos = jnp.where(column[None, :] < counts[:, None], member, -1).astype(jnp.int32)
    rank_of = jnp.zeros((LENGTH,), jnp.int32).at[sorted_order].set((position - starts[bucket_ids[sorted_order]]).astype(jnp.int32))
    slot_of = (bucket_ids * (N_SEQ * CAP) + rank_of).astype(jnp.int32)
    return (slot_pos, slot_of)

def head_attention(qk_head, value_head, slot_pos, slot_of, length):
    safe_pos = jnp.maximum(slot_pos, 0)
    key_unit = low(qk_head * lax.rsqrt(lax.optimization_barrier(jnp.sum(qk_head * qk_head, axis=-1, keepdims=True)) + KEY_EPS))
    queries = qk_head[safe_pos]
    unit_keys = key_unit[safe_pos]
    values = value_head[safe_pos]
    scores = low_back(jnp.einsum('bic,bjc->bij', queries, unit_keys, precision=PRECISE))
    query_pos = slot_pos[:, :, None]
    key_pos = slot_pos[:, None, :]
    allowed = (key_pos < query_pos) & (key_pos >= 0) & (key_pos < length)
    slot_count = slot_pos.shape[1]
    diagonal = jnp.arange(slot_count)[:, None] == jnp.arange(slot_count)[None, :]
    scores = jnp.where(allowed, scores, jnp.where(diagonal, scores - PENALTY, MASKED))
    log_total = jax.nn.logsumexp(scores, axis=-1)
    probability = jnp.exp(scores - log_total[:, :, None])
    result = low_back(jnp.einsum('bij,bjc->bic', low(probability), values, precision=PRECISE))
    flat_rows = result.reshape(-1, result.shape[-1])
    return (flat_rows[slot_of], log_total.reshape(-1)[slot_of])

def sequence_loss(weights, sequence):
    attn_in, attn_out, ffn_in, ffn_out, tables, norm_params = weights
    tokens, targets, loss_mask, length, buckets = sequence
    position = jnp.arange(LENGTH, dtype=jnp.int32)
    upper_rows = LENGTH // POS_LO
    embedded = tables[tokens] + tables[2 * VOCAB + position // POS_LO]
    embedded = embedded + tables[2 * VOCAB + upper_rows + position % POS_LO]
    normed = low(layer_norm(embedded, norm_params[0], norm_params[1]))
    qk_all = low(low_back(matmul(normed, attn_in[:, 0, :])))
    value_all = low(low_back(matmul(normed, attn_in[:, 1, :])))
    qk_heads = qk_all.reshape(LENGTH, HEADS, HEAD).transpose(1, 0, 2)
    value_heads = value_all.reshape(LENGTH, HEADS, HEAD).transpose(1, 0, 2)
    outputs = []
    totals = []
    for index in range(ROUNDS):
        slot_pos, slot_of = bucket_slots(buckets[index, :, 0])

        def per_head(head_pair, slot_pos=slot_pos, slot_of=slot_of):
            return head_attention(head_pair[0], head_pair[1], slot_pos, slot_of, length)
        result, log_total = lax.map(jax.checkpoint(per_head), (qk_heads, value_heads))
        outputs.append(result)
        totals.append(log_total)
    round_out = jnp.stack(outputs)
    round_lse = jnp.stack(totals)
    mixing = jax.nn.softmax(round_lse, axis=0)
    attended = lax.optimization_barrier(jnp.sum(mixing[..., None] * round_out, axis=0))
    attended = low(low_back(attended.transpose(1, 0, 2).reshape(LENGTH, HEADS * HEAD)))
    first_out = embedded + low_back(matmul(attended, attn_out))
    middle = low(layer_norm(first_out, norm_params[2], norm_params[3]))
    hidden = low(low_back(jax.nn.relu(matmul(middle, ffn_in))))
    second_out = embedded + low_back(matmul(hidden, ffn_out))
    final_rows = low(layer_norm(first_out + second_out, norm_params[4], norm_params[5]))
    logits = low_back(matmul(final_rows, tables[VOCAB:2 * VOCAB].T))
    picked = jnp.take_along_axis(logits, targets[:, None], axis=1)[:, 0]
    bits_lost = (jax.nn.logsumexp(logits, axis=-1) - picked) / LOG_TWO
    live_pos = (loss_mask * (position < length)).astype(jnp.float32)
    live_count = jnp.sum(live_pos)
    return length.astype(jnp.float32) / LENGTH * jnp.sum(live_pos * bits_lost) / live_count

def total_loss(weights, tokens, targets, loss_mask, lengths, buckets):
    rounded = tuple((low(weight) for weight in weights))

    def step_fn(running, sequence):
        return (running + sequence_loss(rounded, sequence), None)
    summed, _ = lax.scan(jax.checkpoint(step_fn), jnp.float32(0.0), (tokens, targets, loss_mask, lengths, buckets))
    return summed

def adam_step(weight, grad_value, moment_one, moment_two, step_rate, clip_scale):
    clipped = grad_value * clip_scale
    new_one = BETA_ONE * moment_one + (1.0 - BETA_ONE) * clipped
    new_two = BETA_TWO * moment_two + (1.0 - BETA_TWO) * clipped * clipped
    fix_one = 1.0 - BETA_ONE ** STEP
    fix_two = 1.0 - BETA_TWO ** STEP
    change = new_one / fix_one / (jnp.sqrt(new_two / fix_two) + ADAM_EPS) + WEIGHT_DECAY * weight
    return (weight - step_rate * change, new_one, new_two)

def reference(attn_in, attn_out, ffn_in, ffn_out, tables, norm_params, m_attn_in, m_attn_out, m_ffn_in, m_ffn_out, m_tables, m_norm_params, v_attn_in, v_attn_out, v_ffn_in, v_ffn_out, v_tables, v_norm_params, tokens, targets, loss_mask, lengths, buckets):
    weights = (attn_in, attn_out, ffn_in, ffn_out, tables, norm_params)
    firsts = (m_attn_in, m_attn_out, m_ffn_in, m_ffn_out, m_tables, m_norm_params)
    seconds = (v_attn_in, v_attn_out, v_ffn_in, v_ffn_out, v_tables, v_norm_params)

    def objective(params):
        return total_loss(params, tokens, targets, loss_mask, lengths, buckets)
    loss_total, pullback = jax.vjp(objective, weights)
    grad_list = pullback(jnp.ones_like(loss_total))[0]
    squares = jnp.float32(0.0)
    for grad_value in grad_list:
        squares = squares + jnp.sum(grad_value * grad_value)
    grad_norm = jnp.sqrt(squares)
    clip_scale = jnp.minimum(1.0, CLIP_NORM / (grad_norm + 1e-06))
    results = [adam_step(weights[index], grad_list[index], firsts[index], seconds[index], STEP_RATES[index], clip_scale) for index in range(6)]
    return (results[0][0], results[1][0], results[2][0], results[3][0], results[4][0], results[5][0], results[0][1], results[1][1], results[2][1], results[3][1], results[4][1], results[5][1], results[0][2], results[1][2], results[2][2], results[3][2], results[4][2], results[5][2], grad_norm, loss_total)
```

```python
import functools

import jax
import jax.numpy as jnp
from jax import lax
from jax.experimental import pallas as pl
from jax.experimental.pallas import tpu as pltpu
from jax.sharding import Mesh
from jax.sharding import PartitionSpec as P

HEAD = 128
VOCAB = 256
BUCKETS = 256
POS_LO = 128
STEP = 10


PENALTY = 10000.0
MASKED = -1000000000.0
LN_EPS = 1e-05
KEY_EPS = 1e-06
CLIP_NORM = 0.05
BETA_ONE = 0.9
BETA_TWO = 0.999
ADAM_EPS = 1e-08
WEIGHT_DECAY = 0.01
STEP_RATES = (0.1, 0.2, 0.1, 0.05, 0.5, 0.5)
LOG_TWO = 0.6931471805599453

CHIPS = ("pair", "sub")
SEQ = ("pair", "sub", "core")
ALL = ("pair", "sub", "core", "ffn")
F32 = jnp.float32
BF16 = jnp.bfloat16


def norm_forward(values, scale_row, shift_row):
    average = jnp.mean(values, axis=-1, keepdims=True)
    centred = values - average
    inv_std = lax.rsqrt(jnp.mean(centred * centred, axis=-1, keepdims=True) + LN_EPS)
    normal_part = centred * inv_std
    return (normal_part * scale_row + shift_row, normal_part, inv_std)


def norm_backward(upstream, normal_part, inv_std, scale_row):
    axes_list = tuple(range(upstream.ndim - 1))
    grad_scale = jnp.sum(upstream * normal_part, axis=axes_list)
    grad_shift = jnp.sum(upstream, axis=axes_list)
    scaled = upstream * scale_row
    grad_input = inv_std * (
        scaled
        - jnp.mean(scaled, axis=-1, keepdims=True)
        - normal_part * jnp.mean(scaled * normal_part, axis=-1, keepdims=True)
    )
    return (grad_input, grad_scale, grad_shift)


def adam_step(weight, grad_value, moment_one, moment_two, step_rate, clip_scale):
    clipped = grad_value * clip_scale
    new_one = BETA_ONE * moment_one + (1.0 - BETA_ONE) * clipped
    new_two = BETA_TWO * moment_two + (1.0 - BETA_TWO) * clipped * clipped
    fix_one = 1.0 - BETA_ONE**STEP
    fix_two = 1.0 - BETA_TWO**STEP
    change = new_one / fix_one / (jnp.sqrt(new_two / fix_two) + ADAM_EPS) + WEIGHT_DECAY * weight
    return (weight - step_rate * change, new_one, new_two)


def swap_core(values):
    return lax.ppermute(values, "core", [(0, 1), (1, 0)])


def spread_all(piece, axes):
    count = lax.axis_size(axes)
    copies = jnp.broadcast_to(piece[None], (count,) + piece.shape)
    own = lax.all_to_all(copies, axes, 0, 0, tiled=True)
    other = swap_core(own)
    first = lax.axis_index("core") == 0
    return jnp.where(first, jnp.stack([own, other], 1), jnp.stack([other, own], 1))


def sum_scatter(values, axes):
    core = lax.axis_index("core")
    keep = lax.dynamic_index_in_dim(values, core, 1, keepdims=False)
    give = lax.dynamic_index_in_dim(values, 1 - core, 1, keepdims=False)
    both = keep + swap_core(give.astype(BF16)).astype(F32)
    moved = lax.all_to_all(both.astype(BF16), axes, 0, 0, tiled=True)
    return jnp.sum(moved.astype(F32), axis=0)


def total_of(value):
    count = lax.axis_size(ALL)
    row = jnp.broadcast_to(value[None], (count,) + value.shape)
    return jnp.sum(lax.all_to_all(row, ALL, 0, 0, tiled=True), axis=0)


CONTRACT_LAST = (((1,), (1,)), ((), ()))
CONTRACT_FIRST = (((0,), (0,)), ((), ()))
PLAIN = (((1,), (0,)), ((), ()))


def mm(left, right, dims):
    return lax.dot_general(left, right, dims, preferred_element_type=F32)


def pair_counts(key_ids, query_ids, rounds):
    total = None
    for r in range(rounds):
        same = jnp.where(key_ids[:, r : r + 1] == query_ids[r : r + 1, :], 1.0, 0.0)
        total = same if total is None else total + same
    return total


def own_block(scores, counts, rounds):
    keys = lax.broadcasted_iota(jnp.int32, scores.shape, 0)
    queries = lax.broadcasted_iota(jnp.int32, scores.shape, 1)
    itself = keys == queries
    counts = jnp.where(itself, float(rounds), jnp.where(keys < queries, counts, 0.0))
    return jnp.where(itself, scores - PENALTY, scores), counts


def forward_kernel(
    rounds, info_ref, rows_ref, key_id_ref, query_id_ref, out_ref, wide_ref, stat_ref, unit_ref
):
    halves, pairs, seg = rows_ref.shape[:3]
    half = info_ref[0]

    def unit(step, carry):
        slot, pair = step // pairs, step % pairs
        rows = rows_ref[slot, pair, :, :HEAD].astype(F32)
        scale = lax.rsqrt(jnp.sum(rows * rows, axis=-1, keepdims=True) + KEY_EPS)
        unit_ref[slot, pair] = (rows * scale).astype(BF16)
        return carry

    lax.fori_loop(0, halves * pairs, unit, 0)

    def query_block(pair, carry):
        block = pair * halves + half
        own_slot = info_ref[1 + half]
        queries = rows_ref[own_slot, pair, :, :HEAD]
        query_ids = query_id_ref[block]

        def visit(index, state, diagonal):
            top, total, acc = state
            key_pair, slot = index // halves, info_ref[1 + index % halves]
            scores = mm(unit_ref[slot, key_pair], queries, CONTRACT_LAST)
            counts = pair_counts(key_id_ref[index], query_ids, rounds)
            if diagonal:
                scores, counts = own_block(scores, counts, rounds)
            new_top = jnp.maximum(
                top, jnp.max(jnp.where(counts > 0.0, scores, MASKED), axis=0, keepdims=True)
            )
            weights = jnp.where(counts > 0.0, jnp.exp(scores - new_top) * counts, 0.0)
            fade = jnp.exp(top - new_top)
            total = fade * total + jnp.sum(weights, axis=0, keepdims=True)
            values = rows_ref[slot, key_pair, :, HEAD:]
            acc = fade * acc + mm(values, weights.astype(BF16), CONTRACT_FIRST)
            return new_top, total, acc

        start = (
            jnp.full((1, seg), MASKED, F32),
            jnp.zeros((1, seg), F32),
            jnp.zeros((HEAD, seg), F32),
        )
        state = visit(block, start, True)
        top, total, acc = lax.fori_loop(
            0, block, lambda index, held: visit(index, held, False), state
        )
        inverse = 1.0 / total
        result = jnp.transpose(acc * inverse)
        out_ref[pair] = result.astype(BF16)
        wide_ref[pair] = result
        stat_ref[pair, 0:1, :] = top
        stat_ref[pair, 1:2, :] = inverse
        return carry

    lax.fori_loop(0, pairs, query_block, 0)


def backward_kernel(
    rounds,
    info_ref,
    rows_ref,
    key_id_ref,
    query_id_ref,
    unit_ref,
    grad_ref,
    wide_ref,
    stat_ref,
    query_grad_ref,
    key_grad_ref,
    value_grad_ref,
):
    halves, pairs, seg = rows_ref.shape[:3]
    half = info_ref[0]

    def clear(step, carry):
        zero = jnp.zeros((seg, HEAD), F32)
        key_grad_ref[step // pairs, step % pairs] = zero
        value_grad_ref[step // pairs, step % pairs] = zero
        return carry

    lax.fori_loop(0, halves * pairs, clear, 0)

    def query_block(pair, carry):
        block = pair * halves + half
        own_slot = info_ref[1 + half]
        queries = rows_ref[own_slot, pair, :, :HEAD]
        query_ids = query_id_ref[block]
        grads = grad_ref[pair]
        spent = grads.astype(F32) * wide_ref[pair]
        inner = jnp.sum(jnp.transpose(spent), axis=0, keepdims=True)
        top = stat_ref[pair, 0:1, :]
        inverse = stat_ref[pair, 1:2, :]

        def visit(index, acc, diagonal):
            key_pair, slot = index // halves, info_ref[1 + index % halves]
            keys = unit_ref[slot, key_pair]
            scores = mm(keys, queries, CONTRACT_LAST)
            counts = pair_counts(key_id_ref[index], query_ids, rounds)
            if diagonal:
                scores, counts = own_block(scores, counts, rounds)
            weights = jnp.where(counts > 0.0, jnp.exp(scores - top) * (counts * inverse), 0.0)
            value_grad_ref[slot, key_pair] += mm(weights.astype(BF16), grads, PLAIN)
            grad_weights = mm(rows_ref[slot, key_pair, :, HEAD:], grads, CONTRACT_LAST)
            grad_scores = (weights * (grad_weights - inner)).astype(BF16)
            key_grad_ref[slot, key_pair] += mm(grad_scores, queries, PLAIN)
            return acc + mm(keys, grad_scores, CONTRACT_FIRST)

        acc = visit(block, jnp.zeros((HEAD, seg), F32), True)
        acc = lax.fori_loop(0, block, lambda index, held: visit(index, held, False), acc)
        query_grad_ref[pair] = jnp.transpose(acc)
        return carry

    lax.fori_loop(0, pairs, query_block, 0)


def in_vmem(count):
    return [pl.BlockSpec(memory_space=pltpu.VMEM)] * count


def attend(info, rows, key_ids, query_ids, rounds):
    halves, pairs, seg = rows.shape[:3]
    return pl.pallas_call(
        functools.partial(forward_kernel, rounds),
        out_shape=(
            jax.ShapeDtypeStruct((pairs, seg, HEAD), BF16),
            jax.ShapeDtypeStruct((pairs, seg, HEAD), F32),
            jax.ShapeDtypeStruct((pairs, 2, seg), F32),
            jax.ShapeDtypeStruct((halves, pairs, seg, HEAD), BF16),
        ),
        in_specs=[pl.BlockSpec(memory_space=pltpu.SMEM)] + in_vmem(3),
        out_specs=tuple(in_vmem(4)),
        compiler_params=pltpu.CompilerParams(vmem_limit_bytes=56 << 20),
        name="attend",
    )(info, rows, key_ids, query_ids)


def attend_back(info, rows, key_ids, query_ids, unit, grads, wide, stats, rounds):
    halves, pairs, seg = rows.shape[:3]
    return pl.pallas_call(
        functools.partial(backward_kernel, rounds),
        out_shape=(
            jax.ShapeDtypeStruct((pairs, seg, HEAD), F32),
            jax.ShapeDtypeStruct((halves, pairs, seg, HEAD), F32),
            jax.ShapeDtypeStruct((halves, pairs, seg, HEAD), F32),
        ),
        in_specs=[pl.BlockSpec(memory_space=pltpu.SMEM)] + in_vmem(7),
        out_specs=tuple(in_vmem(3)),
        compiler_params=pltpu.CompilerParams(vmem_limit_bytes=56 << 20),
        name="attend_back",
    )(info, rows, key_ids, query_ids, unit, grads, wide, stats)


def per_device(
    attn_in,
    attn_out,
    ffn_in,
    ffn_out,
    tables,
    norm_params,
    m_attn_in,
    m_attn_out,
    m_ffn_in,
    m_ffn_out,
    m_tables,
    m_norm_params,
    v_attn_in,
    v_attn_out,
    v_ffn_in,
    v_ffn_out,
    v_tables,
    v_norm_params,
    tokens,
    targets,
    loss_mask,
    lengths,
    buckets,
):
    pairs, subs, cores, n_ffn = (lax.axis_size(axis) for axis in ALL)
    halves = subs * cores
    n_seq = pairs * halves
    chips = pairs * subs
    pair_rank = lax.axis_index("pair")
    half_rank = lax.axis_index("sub") * cores + lax.axis_index("core")
    seq_rank = pair_rank * halves + half_rank
    ffn_rank = lax.axis_index("ffn")
    num_seqs, seg_len = tokens.shape
    sub_len = targets.shape[1]
    full_len = loss_mask.shape[1]
    rounds = buckets.shape[1]
    upper_rows = full_len // POS_LO
    rows_total = tables.shape[0]
    slice_cols = tables.shape[1]
    width = slice_cols * n_seq * n_ffn
    head_width = attn_in.shape[2]
    heads_local = head_width // HEAD
    hid = ffn_in.shape[1]

    thin = jnp.concatenate([tables, norm_params], axis=0).astype(BF16).T
    thin_all = spread_all(thin, ("pair", "sub", "ffn"))
    thin_all = thin_all.reshape(chips, n_ffn, cores, slice_cols, thin.shape[1])
    thin_all = thin_all.transpose(0, 2, 1, 3, 4).reshape(width, thin.shape[1])
    table_all = thin_all[:, :rows_total]
    norm_rows = thin_all[:, rows_total:].T.astype(F32)
    w_in = spread_all(attn_in.astype(BF16).reshape(-1, 2 * head_width), CHIPS)
    w_in = w_in.reshape(width, 2 * head_width)
    w_out = lax.all_gather(attn_out.astype(BF16).T, ("ffn",) + SEQ, axis=0, tiled=True)
    w_out = w_out.reshape(n_ffn, width, head_width)
    w_up = lax.all_gather(ffn_in.astype(BF16), SEQ, axis=0, tiled=True)
    w_down = lax.all_gather(ffn_out.astype(BF16).T, SEQ, axis=0, tiled=True)

    seg_start = seq_rank * seg_len
    position = seg_start + jnp.arange(seg_len, dtype=jnp.int32)
    column = jnp.arange(rows_total, dtype=jnp.int32)
    hot = (
        (column == tokens[..., None])
        | (column == (2 * VOCAB + position // POS_LO)[None, :, None])
        | (column == (2 * VOCAB + upper_rows + position % POS_LO)[None, :, None])
    )
    hot = hot.astype(BF16).reshape(num_seqs * seg_len, rows_total)
    embedded = mm(hot, table_all, CONTRACT_LAST)
    normed_full, normal_one, inv_one = norm_forward(embedded, norm_rows[0], norm_rows[1])
    normed = normed_full.astype(BF16)

    def own_rows(values):
        whole = values.reshape(num_seqs, seg_len, -1)
        return lax.dynamic_slice_in_dim(whole, ffn_rank * sub_len, sub_len, 1).reshape(
            num_seqs * sub_len, -1
        )

    own_embed = own_rows(embedded)

    projected = mm(normed, w_in, PLAIN).astype(BF16)
    projected = projected.reshape(num_seqs, seg_len, 2, heads_local, HEAD)
    projected = projected.transpose(0, 3, 1, 2, 4).reshape(pairs, seg_len, 2 * HEAD)
    own = lax.all_to_all(projected, "pair", 0, 0, tiled=True)
    if subs == 1:
        rows = jnp.stack([own, swap_core(own)])
        slots = jnp.arange(halves, dtype=jnp.int32) ^ half_rank
    else:
        rows = lax.all_gather(own, ("sub", "core"), axis=0, tiled=False)
        slots = jnp.arange(halves, dtype=jnp.int32)
    info = jnp.concatenate([half_rank[None].astype(jnp.int32), slots.astype(jnp.int32)])
    my_seq = pair_rank // heads_local
    my_ids = lax.dynamic_index_in_dim(buckets[..., 0], my_seq, 0, keepdims=False)
    my_length = lax.dynamic_index_in_dim(lengths, my_seq, 0, keepdims=False)
    query_ids = my_ids.reshape(rounds, n_seq, seg_len).transpose(1, 0, 2)
    usable = jnp.arange(full_len, dtype=jnp.int32) < my_length
    key_ids = jnp.where(usable[:, None], my_ids.T, -1).reshape(n_seq, seg_len, rounds)
    out, wide, stats, unit = attend(info, rows, key_ids, query_ids, rounds)

    both = ("pair", "ffn")
    moved = lax.all_to_all(
        out.reshape(pairs * n_ffn, sub_len, HEAD), both, 0, 0, tiled=True
    )
    moved = moved.reshape(num_seqs, heads_local, n_ffn, sub_len, HEAD)
    attended = moved.transpose(0, 3, 2, 1, 4).reshape(num_seqs * sub_len, n_ffn, head_width)
    branch = jnp.einsum("rzc,zdc->rd", attended, w_out, preferred_element_type=F32)

    def whole_rows(values):
        split = values.reshape(num_seqs, sub_len, -1)
        return lax.all_gather(split, "ffn", axis=1, tiled=True).reshape(num_seqs * seg_len, -1)

    def share_rows(values):
        split = values.astype(BF16).reshape(num_seqs, seg_len, -1)
        return (
            lax.psum_scatter(split, "ffn", scatter_dimension=1, tiled=True)
            .reshape(num_seqs * sub_len, -1)
            .astype(F32)
        )

    first_out = own_embed + branch
    middle_own, normal_two, inv_two = norm_forward(first_out, norm_rows[2], norm_rows[3])
    middle = whole_rows(middle_own.astype(BF16))
    pre_act = mm(middle, w_up, PLAIN)
    hidden = jnp.maximum(pre_act, 0.0).astype(BF16)
    second_out = own_embed + share_rows(mm(hidden, w_down, CONTRACT_LAST))
    final_full, normal_three, inv_three = norm_forward(
        first_out + second_out, norm_rows[4], norm_rows[5]
    )
    final_rows = final_full.astype(BF16)

    head_cols = table_all[:, VOCAB : 2 * VOCAB]
    logits = mm(final_rows, head_cols, PLAIN)
    log_norm = jax.nn.logsumexp(logits, axis=-1)
    wanted = targets.reshape(num_seqs * sub_len)
    target_hot = (wanted[:, None] == jnp.arange(VOCAB, dtype=jnp.int32)).astype(F32)
    picked = jnp.sum(logits * target_hot, axis=-1)
    bits_lost = (log_norm - picked) / LOG_TWO
    live_all = (
        loss_mask * (jnp.arange(full_len, dtype=jnp.int32)[None, :] < lengths[:, None])
    ).astype(F32)
    counts = jnp.sum(live_all, axis=1)
    live_own = lax.dynamic_slice_in_dim(live_all, seg_start + ffn_rank * sub_len, sub_len, 1)
    weight_row = lengths.astype(F32) / full_len / counts
    loss_weight = (live_own * weight_row[:, None]).reshape(num_seqs * sub_len)
    loss_part = jnp.sum(loss_weight * bits_lost)
    softmax_p = jnp.exp(logits - log_norm[:, None])
    grad_logits = ((loss_weight / LOG_TWO)[:, None] * (softmax_p - target_hot)).astype(BF16)
    grad_final = mm(grad_logits, head_cols, CONTRACT_LAST)
    grad_head = mm(final_rows, grad_logits, CONTRACT_FIRST)
    grad_sum, gain_five, bias_five = norm_backward(
        grad_final, normal_three, inv_three, norm_rows[4]
    )

    rows_grad = whole_rows(grad_sum.astype(BF16))
    grad_hidden = mm(rows_grad, w_down, PLAIN)
    grad_pre = jnp.where(pre_act > 0.0, grad_hidden, 0.0).astype(BF16)
    grad_middle = share_rows(mm(grad_pre, w_up, CONTRACT_LAST))
    grad_down = mm(rows_grad, hidden, CONTRACT_FIRST)
    grad_up = mm(middle, grad_pre, CONTRACT_FIRST)
    first_part, gain_three, bias_three = norm_backward(
        grad_middle, normal_two, inv_two, norm_rows[2]
    )
    grad_first = first_part + grad_sum

    grad_branch = grad_first.astype(BF16)
    grad_out = jnp.einsum("rzc,rd->zdc", attended, grad_branch, preferred_element_type=F32)
    grad_att = jnp.einsum("rd,zdc->rzc", grad_branch, w_out, preferred_element_type=F32)
    grad_att = grad_att.astype(BF16).reshape(num_seqs, sub_len, n_ffn, heads_local, HEAD)
    grad_att = grad_att.transpose(0, 3, 2, 1, 4).reshape(pairs * n_ffn, sub_len, HEAD)
    grads = lax.all_to_all(grad_att, both, 0, 0, tiled=True).reshape(pairs, seg_len, HEAD)
    query_grad, key_grad, value_grad = attend_back(
        info, rows, key_ids, query_ids, unit, grads, wide, stats, rounds
    )
    if subs == 1:
        away = jnp.concatenate([key_grad[1], value_grad[1]], axis=-1).astype(BF16)
        came = swap_core(away).astype(F32)
        keys_total = key_grad[0] + came[..., :HEAD]
        values_total = value_grad[0] + came[..., HEAD:]
    else:
        away = jnp.concatenate([key_grad, value_grad], axis=-1).astype(BF16)
        came = lax.psum_scatter(away, ("sub", "core"), scatter_dimension=0).astype(F32)
        keys_total, values_total = came[..., :HEAD], came[..., HEAD:]
    widened = own[..., :HEAD].astype(F32)
    inv_norm = lax.rsqrt(jnp.sum(widened * widened, axis=-1, keepdims=True) + KEY_EPS)
    grad_qk = (
        query_grad
        + keys_total * inv_norm
        - widened * inv_norm**3 * jnp.sum(widened * keys_total, axis=-1, keepdims=True)
    )
    owner_grads = jnp.concatenate([grad_qk, values_total], axis=-1).astype(BF16)
    grad_proj = lax.all_to_all(owner_grads, "pair", 0, 0, tiled=True)
    grad_proj = grad_proj.reshape(num_seqs, heads_local, seg_len, 2, HEAD)
    grad_proj = grad_proj.transpose(0, 2, 3, 1, 4).reshape(num_seqs * seg_len, 2 * head_width)
    grad_in = mm(normed, grad_proj, CONTRACT_FIRST)
    grad_normed = mm(grad_proj, w_in, CONTRACT_LAST)
    embed_part, gain_one, bias_one = norm_backward(grad_normed, normal_one, inv_one, norm_rows[0])
    whole = embed_part.reshape(num_seqs, seg_len, width)
    extra = (grad_first + grad_sum).reshape(num_seqs, sub_len, width)
    own_total = lax.dynamic_slice_in_dim(whole, ffn_rank * sub_len, sub_len, 1) + extra
    whole = lax.dynamic_update_slice_in_dim(whole, own_total, ffn_rank * sub_len, 1)
    embed_grad = whole.reshape(num_seqs * seg_len, width).astype(BF16)
    grad_tables = mm(embed_grad, hot, CONTRACT_FIRST)
    grad_tables = grad_tables + jnp.pad(
        grad_head, ((0, 0), (VOCAB, rows_total - 2 * VOCAB))
    )
    grad_norms = jnp.stack(
        [gain_one, bias_one, gain_three, bias_three, gain_five, bias_five], axis=1
    )

    thin_grad = jnp.concatenate([grad_tables, grad_norms], axis=1)
    thin_grad = thin_grad.reshape(chips, cores, n_ffn, slice_cols, -1).transpose(0, 2, 1, 3, 4)
    thin_grad = sum_scatter(
        thin_grad.reshape(chips * n_ffn, cores, slice_cols, -1), ("pair", "sub", "ffn")
    ).T
    table_grad, norm_grad = thin_grad[:rows_total], thin_grad[rows_total:]
    in_grad = sum_scatter(grad_in.reshape(chips, cores, -1, 2 * head_width), CHIPS)
    in_grad = in_grad.reshape(attn_in.shape)
    out_grad = lax.psum_scatter(
        grad_out.astype(BF16).reshape(n_ffn * width, head_width),
        ("ffn",) + SEQ,
        scatter_dimension=0,
        tiled=True,
    )
    out_grad = out_grad.astype(F32).T
    up_grad = sum_scatter(grad_up.reshape(chips, cores, -1, hid), CHIPS)
    down_grad = sum_scatter(grad_down.reshape(chips, cores, -1, hid), CHIPS).T

    grad_list = (in_grad, out_grad, up_grad, down_grad, table_grad, norm_grad)
    local_sq = jnp.float32(0.0)
    for grad_piece in grad_list:
        local_sq = local_sq + jnp.sum(grad_piece * grad_piece)
    totals = total_of(jnp.stack([local_sq, loss_part]))
    total_sq, loss_total = totals[0], totals[1]
    grad_norm = jnp.sqrt(total_sq)
    clip_scale = jnp.minimum(1.0, CLIP_NORM / (grad_norm + 1e-06))
    weights = (attn_in, attn_out, ffn_in, ffn_out, tables, norm_params)
    firsts = (m_attn_in, m_attn_out, m_ffn_in, m_ffn_out, m_tables, m_norm_params)
    seconds = (v_attn_in, v_attn_out, v_ffn_in, v_ffn_out, v_tables, v_norm_params)
    results = [
        adam_step(
            weights[index],
            grad_list[index],
            firsts[index],
            seconds[index],
            STEP_RATES[index],
            clip_scale,
        )
        for index in range(6)
    ]
    return tuple(results[index][part] for part in range(3) for index in range(6)) + (
        grad_norm,
        loss_total,
    )


def solution(mesh):
    n_seq, n_ffn = mesh.shape["seq"], mesh.shape["ffn"]

    def step(*args):
        num_pairs = args[18].shape[0] * (args[0].shape[2] // HEAD // n_ffn)
        subs = n_seq // 2 // num_pairs
        fine = Mesh(mesh.devices.reshape(num_pairs, subs, 2, n_ffn), ALL)
        weights = (
            P(SEQ, None, "ffn"),
            P("ffn", SEQ),
            P(SEQ, "ffn"),
            P("ffn", SEQ),
            P(None, ALL),
            P(None, ALL),
        )
        return jax.shard_map(
            per_device,
            mesh=fine,
            in_specs=weights * 3 + (P(None, SEQ), P(None, ALL), P(), P(), P()),
            out_specs=weights * 3 + (P(), P()),
            check_vma=False,
        )(*args)

    return step
```

```python
import functools

import jax
import jax.numpy as jnp
from jax import lax
from jax.experimental import pallas as pl
from jax.experimental.pallas import tpu as pltpu
from jax.sharding import Mesh
from jax.sharding import PartitionSpec as P

HEAD = 128
VOCAB = 256
BUCKETS = 256
POS_LO = 128
STEP = 10


PENALTY = 10000.0
MASKED = -1000000000.0
LN_EPS = 1e-05
KEY_EPS = 1e-06
CLIP_NORM = 0.05
BETA_ONE = 0.9
BETA_TWO = 0.999
ADAM_EPS = 1e-08
WEIGHT_DECAY = 0.01
STEP_RATES = (0.1, 0.2, 0.1, 0.05, 0.5, 0.5)
LOG_TWO = 0.6931471805599453

CHIPS = ("p", "a", "b")
SEQ = ("p", "a", "b", "core")
ALL = ("p", "a", "b", "core", "ffn")
GROUP = ("b", "core")
F32 = jnp.float32
BF16 = jnp.bfloat16


def norm_forward(values, scale_row, shift_row):
    average = jnp.mean(values, axis=-1, keepdims=True)
    centred = values - average
    inv_std = lax.rsqrt(jnp.mean(centred * centred, axis=-1, keepdims=True) + LN_EPS)
    normal_part = centred * inv_std
    return (normal_part * scale_row + shift_row, normal_part, inv_std)


def norm_backward(upstream, normal_part, inv_std, scale_row):
    axes_list = tuple(range(upstream.ndim - 1))
    grad_scale = jnp.sum(upstream * normal_part, axis=axes_list)
    grad_shift = jnp.sum(upstream, axis=axes_list)
    scaled = upstream * scale_row
    grad_input = inv_std * (
        scaled
        - jnp.mean(scaled, axis=-1, keepdims=True)
        - normal_part * jnp.mean(scaled * normal_part, axis=-1, keepdims=True)
    )
    return (grad_input, grad_scale, grad_shift)


def adam_step(weight, grad_value, moment_one, moment_two, step_rate, clip_scale):
    clipped = grad_value * clip_scale
    new_one = BETA_ONE * moment_one + (1.0 - BETA_ONE) * clipped
    new_two = BETA_TWO * moment_two + (1.0 - BETA_TWO) * clipped * clipped
    fix_one = 1.0 - BETA_ONE**STEP
    fix_two = 1.0 - BETA_TWO**STEP
    change = new_one / fix_one / (jnp.sqrt(new_two / fix_two) + ADAM_EPS) + WEIGHT_DECAY * weight
    return (weight - step_rate * change, new_one, new_two)


def swap(values, axis):
    return lax.ppermute(values, axis, [(0, 1), (1, 0)])


def swap_core(values):
    return swap(values, "core")


def spread_all(piece, axes):
    count = lax.axis_size(axes)
    copies = jnp.broadcast_to(piece[None], (count,) + piece.shape)
    own = lax.all_to_all(copies, axes, 0, 0, tiled=True)
    other = swap_core(own)
    first = lax.axis_index("core") == 0
    return jnp.where(first, jnp.stack([own, other], 1), jnp.stack([other, own], 1))


def sum_scatter(values, axes):
    core = lax.axis_index("core")
    keep = lax.dynamic_index_in_dim(values, core, 1, keepdims=False)
    give = lax.dynamic_index_in_dim(values, 1 - core, 1, keepdims=False)
    both = keep + swap_core(give.astype(BF16)).astype(F32)
    moved = lax.all_to_all(both.astype(BF16), axes, 0, 0, tiled=True)
    return jnp.sum(moved.astype(F32), axis=0)


def group_rows(values):
    near = jnp.stack([values, swap(values, "b")])
    return jnp.concatenate([near, swap_core(near)]).reshape(-1, values.shape[1])


def group_share(values):
    parts = values.reshape(4, -1, values.shape[1])
    near = parts[:2] + swap_core(parts[2:].astype(BF16)).astype(F32)
    return near[0] + swap(near[1].astype(BF16), "b").astype(F32)


def group_weight(pieces, n_ffn):
    count, depth, hid = pieces.shape
    moved = pieces.reshape(count, depth, 4, hid // 4).transpose(2, 0, 1, 3)
    moved = lax.all_to_all(moved, GROUP, 0, 0, tiled=True)
    whole = lax.all_gather(moved, ("ffn", "p", "a"), axis=0, tiled=False)
    whole = whole.reshape(n_ffn, -1, count, depth, hid // 4).transpose(2, 1, 3, 0, 4)
    return whole.reshape(count, -1, n_ffn * hid // 4)


def group_scatter(grad, n_ffn, depth):
    hid = grad.shape[1] // n_ffn
    middle = lax.axis_size("a")
    parts = grad.reshape(2, middle, 4 * depth, n_ffn, hid).transpose(0, 1, 3, 2, 4)
    side = lax.axis_index("p")
    keep = lax.dynamic_index_in_dim(parts, side, 0, keepdims=False)
    give = lax.dynamic_index_in_dim(parts, 1 - side, 0, keepdims=False)
    both = keep + swap(give.astype(BF16), "p").astype(F32)
    both = both.astype(BF16).reshape(middle * n_ffn, 4, depth, hid)
    moved = lax.all_to_all(both, ("a", "ffn"), 0, 0, tiled=True)
    total = jnp.sum(moved.astype(F32), axis=0).astype(BF16)
    back = lax.all_to_all(total, GROUP, 0, 0, tiled=True)
    return back.astype(F32).transpose(1, 0, 2).reshape(depth, 4 * hid)


def total_of(value):
    count = lax.axis_size(ALL)
    row = jnp.broadcast_to(value[None], (count,) + value.shape)
    return jnp.sum(lax.all_to_all(row, ALL, 0, 0, tiled=True), axis=0)


CONTRACT_LAST = (((1,), (1,)), ((), ()))
CONTRACT_FIRST = (((0,), (0,)), ((), ()))
PLAIN = (((1,), (0,)), ((), ()))


def mm(left, right, dims):
    return lax.dot_general(left, right, dims, preferred_element_type=F32)


def pair_counts(key_ids, query_ids, rounds):
    total = None
    for r in range(rounds):
        same = jnp.where(key_ids[:, r : r + 1] == query_ids[r : r + 1, :], 1.0, 0.0)
        total = same if total is None else total + same
    return total


def own_block(scores, counts, rounds):
    keys = lax.broadcasted_iota(jnp.int32, scores.shape, 0)
    queries = lax.broadcasted_iota(jnp.int32, scores.shape, 1)
    itself = keys == queries
    counts = jnp.where(itself, float(rounds), jnp.where(keys < queries, counts, 0.0))
    return jnp.where(itself, scores - PENALTY, scores), counts


def forward_kernel(
    rounds, info_ref, rows_ref, key_id_ref, query_id_ref, out_ref, wide_ref, stat_ref, unit_ref
):
    halves, pairs, seg = rows_ref.shape[:3]
    half = info_ref[0]

    def unit(step, carry):
        slot, pair = step // pairs, step % pairs
        rows = rows_ref[slot, pair, :, :HEAD].astype(F32)
        scale = lax.rsqrt(jnp.sum(rows * rows, axis=-1, keepdims=True) + KEY_EPS)
        unit_ref[slot, pair] = (rows * scale).astype(BF16)
        return carry

    lax.fori_loop(0, halves * pairs, unit, 0)

    def query_block(pair, carry):
        block = pair * halves + half
        own_slot = info_ref[1 + half]
        queries = rows_ref[own_slot, pair, :, :HEAD]
        query_ids = query_id_ref[block]

        def visit(index, state, diagonal):
            top, total, acc = state
            key_pair, slot = index // halves, info_ref[1 + index % halves]
            scores = mm(unit_ref[slot, key_pair], queries, CONTRACT_LAST)
            counts = pair_counts(key_id_ref[index], query_ids, rounds)
            if diagonal:
                scores, counts = own_block(scores, counts, rounds)
            new_top = jnp.maximum(
                top, jnp.max(jnp.where(counts > 0.0, scores, MASKED), axis=0, keepdims=True)
            )
            weights = jnp.where(counts > 0.0, jnp.exp(scores - new_top) * counts, 0.0)
            fade = jnp.exp(top - new_top)
            total = fade * total + jnp.sum(weights, axis=0, keepdims=True)
            values = rows_ref[slot, key_pair, :, HEAD:]
            acc = fade * acc + mm(values, weights.astype(BF16), CONTRACT_FIRST)
            return new_top, total, acc

        start = (
            jnp.full((1, seg), MASKED, F32),
            jnp.zeros((1, seg), F32),
            jnp.zeros((HEAD, seg), F32),
        )
        state = visit(block, start, True)
        top, total, acc = lax.fori_loop(
            0, block, lambda index, held: visit(index, held, False), state
        )
        inverse = 1.0 / total
        result = jnp.transpose(acc * inverse)
        out_ref[pair] = result.astype(BF16)
        wide_ref[pair] = result
        stat_ref[pair, 0:1, :] = top
        stat_ref[pair, 1:2, :] = inverse
        return carry

    lax.fori_loop(0, pairs, query_block, 0)


def backward_kernel(
    rounds,
    info_ref,
    rows_ref,
    key_id_ref,
    query_id_ref,
    unit_ref,
    grad_ref,
    wide_ref,
    stat_ref,
    query_grad_ref,
    key_grad_ref,
    value_grad_ref,
):
    halves, pairs, seg = rows_ref.shape[:3]
    half = info_ref[0]

    def clear(step, carry):
        zero = jnp.zeros((seg, HEAD), F32)
        key_grad_ref[step // pairs, step % pairs] = zero
        value_grad_ref[step // pairs, step % pairs] = zero
        return carry

    lax.fori_loop(0, halves * pairs, clear, 0)

    def query_block(pair, carry):
        block = pair * halves + half
        own_slot = info_ref[1 + half]
        queries = rows_ref[own_slot, pair, :, :HEAD]
        query_ids = query_id_ref[block]
        grads = grad_ref[pair]
        spent = grads.astype(F32) * wide_ref[pair]
        inner = jnp.sum(jnp.transpose(spent), axis=0, keepdims=True)
        top = stat_ref[pair, 0:1, :]
        inverse = stat_ref[pair, 1:2, :]

        def visit(index, acc, diagonal):
            key_pair, slot = index // halves, info_ref[1 + index % halves]
            keys = unit_ref[slot, key_pair]
            scores = mm(keys, queries, CONTRACT_LAST)
            counts = pair_counts(key_id_ref[index], query_ids, rounds)
            if diagonal:
                scores, counts = own_block(scores, counts, rounds)
            weights = jnp.where(counts > 0.0, jnp.exp(scores - top) * (counts * inverse), 0.0)
            value_grad_ref[slot, key_pair] += mm(weights.astype(BF16), grads, PLAIN)
            grad_weights = mm(rows_ref[slot, key_pair, :, HEAD:], grads, CONTRACT_LAST)
            grad_scores = (weights * (grad_weights - inner)).astype(BF16)
            key_grad_ref[slot, key_pair] += mm(grad_scores, queries, PLAIN)
            return acc + mm(keys, grad_scores, CONTRACT_FIRST)

        acc = visit(block, jnp.zeros((HEAD, seg), F32), True)
        acc = lax.fori_loop(0, block, lambda index, held: visit(index, held, False), acc)
        query_grad_ref[pair] = jnp.transpose(acc)
        return carry

    lax.fori_loop(0, pairs, query_block, 0)


def in_vmem(count):
    return [pl.BlockSpec(memory_space=pltpu.VMEM)] * count


def attend(info, rows, key_ids, query_ids, rounds):
    halves, pairs, seg = rows.shape[:3]
    return pl.pallas_call(
        functools.partial(forward_kernel, rounds),
        out_shape=(
            jax.ShapeDtypeStruct((pairs, seg, HEAD), BF16),
            jax.ShapeDtypeStruct((pairs, seg, HEAD), F32),
            jax.ShapeDtypeStruct((pairs, 2, seg), F32),
            jax.ShapeDtypeStruct((halves, pairs, seg, HEAD), BF16),
        ),
        in_specs=[pl.BlockSpec(memory_space=pltpu.SMEM)] + in_vmem(3),
        out_specs=tuple(in_vmem(4)),
        compiler_params=pltpu.CompilerParams(vmem_limit_bytes=56 << 20),
        name="attend",
    )(info, rows, key_ids, query_ids)


def attend_back(info, rows, key_ids, query_ids, unit, grads, wide, stats, rounds):
    halves, pairs, seg = rows.shape[:3]
    return pl.pallas_call(
        functools.partial(backward_kernel, rounds),
        out_shape=(
            jax.ShapeDtypeStruct((pairs, seg, HEAD), F32),
            jax.ShapeDtypeStruct((halves, pairs, seg, HEAD), F32),
            jax.ShapeDtypeStruct((halves, pairs, seg, HEAD), F32),
        ),
        in_specs=[pl.BlockSpec(memory_space=pltpu.SMEM)] + in_vmem(7),
        out_specs=tuple(in_vmem(3)),
        compiler_params=pltpu.CompilerParams(vmem_limit_bytes=56 << 20),
        name="attend_back",
    )(info, rows, key_ids, query_ids, unit, grads, wide, stats)


def per_device(
    pair_axes,
    half_axes,
    attn_in,
    attn_out,
    ffn_in,
    ffn_out,
    tables,
    norm_params,
    m_attn_in,
    m_attn_out,
    m_ffn_in,
    m_ffn_out,
    m_tables,
    m_norm_params,
    v_attn_in,
    v_attn_out,
    v_ffn_in,
    v_ffn_out,
    v_tables,
    v_norm_params,
    tokens,
    targets,
    loss_mask,
    lengths,
    buckets,
):
    n_ffn = lax.axis_size("ffn")
    cores = lax.axis_size("core")
    pairs, halves = lax.axis_size(pair_axes), lax.axis_size(half_axes)
    n_seq = pairs * halves
    chips = n_seq // cores
    pair_rank = lax.axis_index(pair_axes)
    half_rank = lax.axis_index(half_axes)
    seq_rank = pair_rank * halves + half_rank
    ffn_rank = lax.axis_index("ffn")
    num_seqs, seg_len = tokens.shape
    sub_len = targets.shape[1]
    full_len = loss_mask.shape[1]
    rounds = buckets.shape[1]
    upper_rows = full_len // POS_LO
    rows_total = tables.shape[0]
    slice_cols = tables.shape[1]
    width = slice_cols * n_seq * n_ffn
    head_width = attn_in.shape[2]
    heads_local = head_width // HEAD
    hid = ffn_in.shape[1]

    thin = jnp.concatenate([tables, norm_params], axis=0).astype(BF16).T
    thin_all = spread_all(thin, CHIPS + ("ffn",))
    thin_all = thin_all.reshape(chips, n_ffn, cores, slice_cols, thin.shape[1])
    thin_all = thin_all.transpose(0, 2, 1, 3, 4).reshape(width, thin.shape[1])
    table_all = thin_all[:, :rows_total]
    norm_rows = thin_all[:, rows_total:].T.astype(F32)
    w_in = spread_all(attn_in.astype(BF16).reshape(-1, 2 * head_width), CHIPS)
    w_in = w_in.reshape(width, 2 * head_width)
    w_out = lax.all_gather(attn_out.astype(BF16).T, ("ffn",) + SEQ, axis=0, tiled=True)
    w_out = w_out.reshape(n_ffn, width, head_width)
    w_up, w_down = group_weight(jnp.stack([ffn_in, ffn_out.T]).astype(BF16), n_ffn)

    seg_start = seq_rank * seg_len
    position = seg_start + jnp.arange(seg_len, dtype=jnp.int32)
    column = jnp.arange(rows_total, dtype=jnp.int32)
    hot = (
        (column == tokens[..., None])
        | (column == (2 * VOCAB + position // POS_LO)[None, :, None])
        | (column == (2 * VOCAB + upper_rows + position % POS_LO)[None, :, None])
    )
    hot = hot.astype(BF16).reshape(num_seqs * seg_len, rows_total)
    embedded = mm(hot, table_all, CONTRACT_LAST)
    normed_full, normal_one, inv_one = norm_forward(embedded, norm_rows[0], norm_rows[1])
    normed = normed_full.astype(BF16)

    def own_rows(values):
        whole = values.reshape(num_seqs, seg_len, -1)
        return lax.dynamic_slice_in_dim(whole, ffn_rank * sub_len, sub_len, 1).reshape(
            num_seqs * sub_len, -1
        )

    own_embed = own_rows(embedded)

    projected = mm(normed, w_in, PLAIN).astype(BF16)
    projected = projected.reshape(num_seqs, seg_len, 2, heads_local, HEAD)
    projected = projected.transpose(0, 3, 1, 2, 4).reshape(pairs, seg_len, 2 * HEAD)
    own = lax.all_to_all(projected, pair_axes, 0, 0, tiled=True)
    if halves == cores:
        rows = jnp.stack([own, swap_core(own)])
        slots = jnp.arange(halves, dtype=jnp.int32) ^ half_rank
    else:
        rows = lax.all_gather(own, half_axes, axis=0, tiled=False)
        slots = jnp.arange(halves, dtype=jnp.int32)
    info = jnp.concatenate([half_rank[None].astype(jnp.int32), slots.astype(jnp.int32)])
    my_seq = pair_rank // heads_local
    my_ids = lax.dynamic_index_in_dim(buckets[..., 0], my_seq, 0, keepdims=False)
    my_length = lax.dynamic_index_in_dim(lengths, my_seq, 0, keepdims=False)
    query_ids = my_ids.reshape(rounds, n_seq, seg_len).transpose(1, 0, 2)
    usable = jnp.arange(full_len, dtype=jnp.int32) < my_length
    key_ids = jnp.where(usable[:, None], my_ids.T, -1).reshape(n_seq, seg_len, rounds)
    out, wide, stats, unit = attend(info, rows, key_ids, query_ids, rounds)

    both = pair_axes + ("ffn",)
    moved = lax.all_to_all(
        out.reshape(pairs * n_ffn, sub_len, HEAD), both, 0, 0, tiled=True
    )
    moved = moved.reshape(num_seqs, heads_local, n_ffn, sub_len, HEAD)
    attended = moved.transpose(0, 3, 2, 1, 4).reshape(num_seqs * sub_len, n_ffn, head_width)
    branch = jnp.einsum("rzc,zdc->rd", attended, w_out, preferred_element_type=F32)

    first_out = own_embed + branch
    middle_own, normal_two, inv_two = norm_forward(first_out, norm_rows[2], norm_rows[3])
    middle = group_rows(middle_own.astype(BF16))
    pre_act = mm(middle, w_up, PLAIN)
    hidden = jnp.maximum(pre_act, 0.0).astype(BF16)
    second_out = own_embed + group_share(mm(hidden, w_down, CONTRACT_LAST))
    final_full, normal_three, inv_three = norm_forward(
        first_out + second_out, norm_rows[4], norm_rows[5]
    )
    final_rows = final_full.astype(BF16)

    head_cols = table_all[:, VOCAB : 2 * VOCAB]
    logits = mm(final_rows, head_cols, PLAIN)
    log_norm = jax.nn.logsumexp(logits, axis=-1)
    wanted = targets.reshape(num_seqs * sub_len)
    target_hot = (wanted[:, None] == jnp.arange(VOCAB, dtype=jnp.int32)).astype(F32)
    picked = jnp.sum(logits * target_hot, axis=-1)
    bits_lost = (log_norm - picked) / LOG_TWO
    live_all = (
        loss_mask * (jnp.arange(full_len, dtype=jnp.int32)[None, :] < lengths[:, None])
    ).astype(F32)
    counts = jnp.sum(live_all, axis=1)
    live_own = lax.dynamic_slice_in_dim(live_all, seg_start + ffn_rank * sub_len, sub_len, 1)
    weight_row = lengths.astype(F32) / full_len / counts
    loss_weight = (live_own * weight_row[:, None]).reshape(num_seqs * sub_len)
    loss_part = jnp.sum(loss_weight * bits_lost)
    softmax_p = jnp.exp(logits - log_norm[:, None])
    grad_logits = ((loss_weight / LOG_TWO)[:, None] * (softmax_p - target_hot)).astype(BF16)
    grad_final = mm(grad_logits, head_cols, CONTRACT_LAST)
    grad_head = mm(final_rows, grad_logits, CONTRACT_FIRST)
    grad_sum, gain_five, bias_five = norm_backward(
        grad_final, normal_three, inv_three, norm_rows[4]
    )

    rows_grad = group_rows(grad_sum.astype(BF16))
    grad_hidden = mm(rows_grad, w_down, PLAIN)
    grad_pre = jnp.where(pre_act > 0.0, grad_hidden, 0.0).astype(BF16)
    grad_middle = group_share(mm(grad_pre, w_up, CONTRACT_LAST))
    grad_down = mm(rows_grad, hidden, CONTRACT_FIRST)
    grad_up = mm(middle, grad_pre, CONTRACT_FIRST)
    first_part, gain_three, bias_three = norm_backward(
        grad_middle, normal_two, inv_two, norm_rows[2]
    )
    grad_first = first_part + grad_sum

    grad_branch = grad_first.astype(BF16)
    grad_out = jnp.einsum("rzc,rd->zdc", attended, grad_branch, preferred_element_type=F32)
    grad_att = jnp.einsum("rd,zdc->rzc", grad_branch, w_out, preferred_element_type=F32)
    grad_att = grad_att.astype(BF16).reshape(num_seqs, sub_len, n_ffn, heads_local, HEAD)
    grad_att = grad_att.transpose(0, 3, 2, 1, 4).reshape(pairs * n_ffn, sub_len, HEAD)
    grads = lax.all_to_all(grad_att, both, 0, 0, tiled=True).reshape(pairs, seg_len, HEAD)
    query_grad, key_grad, value_grad = attend_back(
        info, rows, key_ids, query_ids, unit, grads, wide, stats, rounds
    )
    if halves == cores:
        away = jnp.concatenate([key_grad[1], value_grad[1]], axis=-1).astype(BF16)
        came = swap_core(away).astype(F32)
        keys_total = key_grad[0] + came[..., :HEAD]
        values_total = value_grad[0] + came[..., HEAD:]
    else:
        away = jnp.concatenate([key_grad, value_grad], axis=-1).astype(BF16)
        came = lax.psum_scatter(away, half_axes, scatter_dimension=0).astype(F32)
        keys_total, values_total = came[..., :HEAD], came[..., HEAD:]
    widened = own[..., :HEAD].astype(F32)
    inv_norm = lax.rsqrt(jnp.sum(widened * widened, axis=-1, keepdims=True) + KEY_EPS)
    grad_qk = (
        query_grad
        + keys_total * inv_norm
        - widened * inv_norm**3 * jnp.sum(widened * keys_total, axis=-1, keepdims=True)
    )
    owner_grads = jnp.concatenate([grad_qk, values_total], axis=-1).astype(BF16)
    grad_proj = lax.all_to_all(owner_grads, pair_axes, 0, 0, tiled=True)
    grad_proj = grad_proj.reshape(num_seqs, heads_local, seg_len, 2, HEAD)
    grad_proj = grad_proj.transpose(0, 2, 3, 1, 4).reshape(num_seqs * seg_len, 2 * head_width)
    grad_in = mm(normed, grad_proj, CONTRACT_FIRST)
    grad_normed = mm(grad_proj, w_in, CONTRACT_LAST)
    embed_part, gain_one, bias_one = norm_backward(grad_normed, normal_one, inv_one, norm_rows[0])
    whole = embed_part.reshape(num_seqs, seg_len, width)
    extra = (grad_first + grad_sum).reshape(num_seqs, sub_len, width)
    own_total = lax.dynamic_slice_in_dim(whole, ffn_rank * sub_len, sub_len, 1) + extra
    whole = lax.dynamic_update_slice_in_dim(whole, own_total, ffn_rank * sub_len, 1)
    embed_grad = whole.reshape(num_seqs * seg_len, width).astype(BF16)
    grad_tables = mm(embed_grad, hot, CONTRACT_FIRST)
    grad_tables = grad_tables + jnp.pad(
        grad_head, ((0, 0), (VOCAB, rows_total - 2 * VOCAB))
    )
    grad_norms = jnp.stack(
        [gain_one, bias_one, gain_three, bias_three, gain_five, bias_five], axis=1
    )

    thin_grad = jnp.concatenate([grad_tables, grad_norms], axis=1)
    thin_grad = thin_grad.reshape(chips, cores, n_ffn, slice_cols, -1).transpose(0, 2, 1, 3, 4)
    thin_grad = sum_scatter(
        thin_grad.reshape(chips * n_ffn, cores, slice_cols, -1), CHIPS + ("ffn",)
    ).T
    table_grad, norm_grad = thin_grad[:rows_total], thin_grad[rows_total:]
    in_grad = sum_scatter(grad_in.reshape(chips, cores, -1, 2 * head_width), CHIPS)
    in_grad = in_grad.reshape(attn_in.shape)
    out_grad = grad_out.reshape(n_ffn, chips, cores, -1, head_width).transpose(1, 0, 2, 3, 4)
    out_grad = sum_scatter(
        out_grad.reshape(chips * n_ffn, cores, -1, head_width), CHIPS + ("ffn",)
    ).T
    up_grad = group_scatter(grad_up, n_ffn, ffn_in.shape[0])
    down_grad = group_scatter(grad_down, n_ffn, ffn_in.shape[0]).T

    grad_list = (in_grad, out_grad, up_grad, down_grad, table_grad, norm_grad)
    local_sq = jnp.float32(0.0)
    for grad_piece in grad_list:
        local_sq = local_sq + jnp.sum(grad_piece * grad_piece)
    totals = total_of(jnp.stack([local_sq, loss_part]))
    total_sq, loss_total = totals[0], totals[1]
    grad_norm = jnp.sqrt(total_sq)
    clip_scale = jnp.minimum(1.0, CLIP_NORM / (grad_norm + 1e-06))
    weights = (attn_in, attn_out, ffn_in, ffn_out, tables, norm_params)
    firsts = (m_attn_in, m_attn_out, m_ffn_in, m_ffn_out, m_tables, m_norm_params)
    seconds = (v_attn_in, v_attn_out, v_ffn_in, v_ffn_out, v_tables, v_norm_params)
    results = [
        adam_step(
            weights[index],
            grad_list[index],
            firsts[index],
            seconds[index],
            STEP_RATES[index],
            clip_scale,
        )
        for index in range(6)
    ]
    return tuple(results[index][part] for part in range(3) for index in range(6)) + (
        grad_norm,
        loss_total,
    )


def solution(mesh):
    n_seq, n_ffn = mesh.shape["seq"], mesh.shape["ffn"]

    def step(*args):
        num_pairs = args[18].shape[0] * (args[0].shape[2] // HEAD // n_ffn)
        fine = Mesh(mesh.devices.reshape(2, n_seq // 8, 2, 2, n_ffn), ALL)
        if num_pairs == n_seq // 2:
            pair_axes, half_axes = CHIPS, ("core",)
        elif num_pairs == 2:
            pair_axes, half_axes = ("p",), ("a", "b", "core")
        else:
            raise ValueError(num_pairs)
        weights = (
            P(SEQ, None, "ffn"),
            P("ffn", SEQ),
            P(SEQ, "ffn"),
            P("ffn", SEQ),
            P(None, ALL),
            P(None, ALL),
        )
        return jax.shard_map(
            functools.partial(per_device, pair_axes, half_axes),
            mesh=fine,
            in_specs=weights * 3 + (P(None, SEQ), P(None, ALL), P(), P(), P()),
            out_specs=weights * 3 + (P(), P()),
            check_vma=False,
        )(*args)

    return step
```
